32 devices in a mesh: row: 4 (over y, x), col: 4 (over z), depth: 2 (over core).
Axes of the slice: x: 2, y: 2, z: 4, core: 2. Of those that a mesh axis runs over, the one named last changes fastest.
Arguments:
- left_outer: bfloat16 [4, 8, 2048, 128], P('row', 'depth', 'col'), may hold values from -6 to 6
- left_inner: bfloat16 [4, 8, 2048, 128], P('row', 'depth', 'col'), may hold values from -0.125 to 0.125
- right_outer: bfloat16 [4, 8, 2048, 128], P('col', 'depth', 'row'), may hold values from -6 to 6
- right_inner: bfloat16 [4, 8, 2048, 128], P('col', 'depth', 'row'), may hold values from -0.125 to 0.125
- range_test: bfloat16 [4, 2048, 128], P('col', 'row'), may hold values from -0.125 to 0.125
- corange_test: bfloat16 [4, 2048, 256], P('row', 'col'), may hold values from -0.125 to 0.125
- product_mask: int32 [4, 4, 8], P('row', 'col', 'depth'), may hold values 0 or 1
Outputs:
- range_factor: float32 [4, 4, 2048, 128], P('row', 'col', 'depth')
- corange_factor: float32 [4, 4, 2048, 128], P('row', 'col', 'depth')
The draws below stay inside these ranges and needn't reach their ends.
All inputs are finite; a program needn't handle non-finite values. No bound on the sum of `product_mask` on one device may be relied on, other than what follows from the above.
Results may differ from the reference program's by a relative error of at most 0.0093.
Values may be sent and summed in bfloat16 or wider, within the bound.
A program may use at most 64 MiB of HBM per device.

```python
import jax
import jax.numpy as jnp
from jax import lax

TILE = 2048
RANK = 128
SKETCH = 256
INNER = 8
TILE_ROWS = 4
TILE_COLS = 4


def with_ends(values, key, low, largest):
    spot = [jax.random.randint(jax.random.fold_in(key, axis), (), 0, length) for axis, length in enumerate(values.shape)]
    main_axis = values.shape.index(max(values.shape))
    neighbour = spot[:main_axis] + [(spot[main_axis] + 1) % values.shape[main_axis]] + spot[main_axis + 1:]
    return values.at[tuple(spot)].set(low).at[tuple(neighbour)].set(largest)


def level_of(key, extent, pieces, low, top_value):
    factor_of, own = 1.0, jax.random.fold_in(key, 6)
    for position, shards_of in pieces:
        heights = jnp.exp(jax.random.uniform(jax.random.fold_in(own, position), (shards_of,), jnp.float32, low / len(pieces), top_value / len(pieces)))
        factor_of = factor_of * jnp.repeat(heights, extent[position] // shards_of).reshape([-1 if axis == position else 1 for axis in range(len(extent))])
    return factor_of


def bell_draw(rng, dims, deviation, limit, shards=(), kind=jnp.bfloat16):
    entries = jax.random.normal(rng, dims, jnp.float32) * deviation
    if len(shards) > 0:
        entries = level_of(rng, dims, shards, -0.22, 0.18) * entries
    return jnp.clip(entries, min=-limit, max=limit).astype(kind)


def setup_inputs(seed: int = 0) -> dict:
    arg_keys = jax.random.split(jax.random.key(seed), 8)
    left_outer = bell_draw(arg_keys[0], (TILE_ROWS, INNER, TILE, RANK), 1.0, 6.0, ((0, 4), (1, 2), (2, 4)))
    left_inner = bell_draw(arg_keys[1], (TILE_ROWS, INNER, TILE, RANK), TILE ** -0.5, 0.125, ((0, 4), (1, 2), (2, 4)))
    right_outer = bell_draw(arg_keys[2], (TILE_COLS, INNER, TILE, RANK), 1.0, 6.0, ((0, 4), (1, 2), (2, 4)))
    right_inner = bell_draw(arg_keys[3], (TILE_COLS, INNER, TILE, RANK), TILE ** -0.5, 0.125, ((0, 4), (1, 2), (2, 4)))
    range_test = bell_draw(arg_keys[4], (TILE_COLS, TILE, RANK), TILE ** -0.5, 0.125, ((0, 4), (1, 4)))
    corange_test = bell_draw(arg_keys[5], (TILE_ROWS, TILE, SKETCH), TILE ** -0.5, 0.125, ((0, 4), (1, 4)))
    product_mask = with_ends((jax.random.randint(arg_keys[6], (TILE_ROWS, TILE_COLS, INNER), 0, 2) < 1).astype(jnp.int32), jax.random.fold_in(arg_keys[6], 1), 0, 1)
    return dict(left_outer=left_outer, left_inner=left_inner, right_outer=right_outer, right_inner=right_inner, range_test=range_test, corange_test=corange_test, product_mask=product_mask)


def reference(left_outer, left_inner, right_outer, right_inner, range_test, corange_test, product_mask):
    flt = jnp.float32
    half = jnp.bfloat16
    highest = lax.Precision.HIGHEST
    scale = INNER ** (-0.5)
    probes = []
    for col_tile in range(TILE_COLS):
        probes.append(jnp.einsum('kbr,bs->krs', right_outer[col_tile].astype(flt), range_test[col_tile].astype(flt)).astype(half))
    tests = []
    for row_tile in range(TILE_ROWS):
        tests.append(jnp.einsum('bs,kbr->ksr', corange_test[row_tile].astype(flt), left_outer[row_tile].astype(flt)).astype(half))
    range_rows = []
    corange_rows = []
    for row_tile in range(TILE_ROWS):
        outer_left = left_outer[row_tile].astype(flt)
        inner_left = left_inner[row_tile].astype(flt)
        test_full = corange_test[row_tile].astype(flt)
        range_line = []
        corange_line = []
        for col_tile in range(TILE_COLS):
            cross = jnp.einsum('kbr,kbs->krs', inner_left, right_inner[col_tile].astype(flt)).astype(half)
            weight = (product_mask[row_tile, col_tile].astype(flt) * scale)[:, None, None]
            core_right = (jnp.einsum('krs,kst->krt', cross.astype(flt), probes[col_tile].astype(flt)) * weight).astype(half)
            core_left = (jnp.einsum('kar,krs->kas', tests[row_tile].astype(flt), cross.astype(flt)) * weight).astype(half)
            range_sketch = jnp.einsum('kbr,krs->bs', outer_left, core_right.astype(flt))
            corange_sketch = jnp.einsum('kbs,kas->ba', right_outer[col_tile].astype(flt), core_left.astype(flt))
            core = jnp.dot(test_full.T, range_sketch, precision=highest)
            gram = jnp.dot(core.T, core, precision=highest)
            ridge = 0.05 * jnp.trace(gram) / RANK + 1e-05
            gram = gram + ridge * jnp.eye(RANK, dtype=flt)
            lower = jnp.linalg.cholesky(gram)
            projected = jnp.dot(corange_sketch, core, precision=highest)
            solved = jax.scipy.linalg.cho_solve((lower, True), projected.T).T
            range_line.append(range_sketch)
            corange_line.append(solved * RANK ** 0.5)
        range_rows.append(jnp.stack(range_line))
        corange_rows.append(jnp.stack(corange_line))
    return (jnp.stack(range_rows), jnp.stack(corange_rows))
```

```python
import functools

import jax
import jax.numpy as jnp
from jax import lax
from jax.experimental import pallas as pl
from jax.experimental.pallas import tpu as pltpu
from jax.sharding import PartitionSpec as P

F32 = jnp.float32
BF16 = jnp.bfloat16
HIGHEST = lax.Precision.HIGHEST
MESH = pl.DeviceIdType.MESH


def mm(a, b, contract=(1, 0), precision=None):
    dims = (((contract[0],), (contract[1],)), ((), ()))
    return lax.dot_general(a, b, dims, precision=precision, preferred_element_type=F32)


def guarded(cond, action):
    if cond is None:
        action()
    else:
        pl.when(cond)(action)


def inverse_schedule(rank):
    low = 1.0 / (rank / 0.05 + 1.0)
    low *= 0.999
    start = 2.0 / (1.0 + low)
    err = 1.0 - low * start
    scales = []
    while err > 1e-8:
        scales.append(2.0 / (2.0 - err * err))
        err = err * err / (2.0 - err * err)
    return start, scales


def kernel(
    sizes,
    lo, li, ro, ri, rt, ct, mask,
    out_range, out_corange,
    lig, rig, pp, ppr, probe, tp, tpr, test, crt, cps, cpr, zz,
    rps, rpr, rsend, rout, qps, qpr, qsend, qout,
    li_l, li_r, li_in, ri_s, ri_in,
    pp_s, pp_in, pr_s, pr_in, tp_s, tp_in, te_s, te_in,
    cr_s, cr_in, cp_s, cp_in, z_s, z_in,
    rp_s, rp_in, ro_s, ro_in, qp_s, qp_in, qo_s, qo_in,
):
    R, C, D, K = sizes
    KR, KC = K // R, K // C
    rank = lo.shape[2]
    r, c, d = lax.axis_index("row"), lax.axis_index("col"), lax.axis_index("depth")
    pending = []

    def copy(src, dst, send, recv, dev, cond=None):
        op = pltpu.make_async_remote_copy(
            src_ref=src, dst_ref=dst, send_sem=send, recv_sem=recv,
            device_id=dev, device_id_type=MESH,
        )
        guarded(cond, op.start)
        pending.append((cond, op))

    def arrive(dst, send, recv, cond=None):
        op = pltpu.make_async_remote_copy(
            src_ref=dst, dst_ref=dst, send_sem=send, recv_sem=recv,
            device_id=(r, c, d), device_id_type=MESH,
        )
        guarded(cond, op.wait_recv)

    def row_peer(o):
        return lax.rem(r + o, R)

    def col_peer(o):
        return lax.rem(c + o, C)

    def depth_peer(o):
        return lax.rem(d + o, D)

    bar = pltpu.get_barrier_semaphore()

    @pl.loop(1, R * D)
    def _(o):
        n = lax.rem(r * D + d + o, R * D)
        pl.semaphore_signal(bar, inc=1, device_id=(n // D, c, lax.rem(n, D)), device_id_type=MESH)

    @pl.loop(1, C * D)
    def _(o):
        n = lax.rem(c * D + d + o, C * D)
        pl.semaphore_signal(bar, inc=1, device_id=(r, n // D, lax.rem(n, D)), device_id_type=MESH)

    pl.semaphore_wait(bar, R * D + C * D - 2)

    def send_li(k):
        copy(li.at[k], lig.at[c, k], li_l.at[0, k], li_in.at[c, k], (r, c - 1, d), c > 0)
        copy(li.at[k], lig.at[c, k], li_r.at[0, k], li_in.at[c, k], (r, c + 1, d), c < C - 1)

    def send_ri(k):
        for o in range(1, R):
            copy(ri.at[k], rig.at[r, k], ri_s.at[o, k], ri_in.at[r, k], (row_peer(o), c, d))

    def forward_li(o, k):
        far = c + o
        cond = far < C
        arrive(lig.at[far, k], li_l.at[o, k], li_in.at[far, k], cond)
        if o < C - 1:
            copy(lig.at[far, k], lig.at[far, k], li_l.at[o, k], li_in.at[far, k],
                 (r, c - 1, d), jnp.logical_and(cond, c > 0))
        near = c - o
        cond = near >= 0
        arrive(lig.at[near, k], li_r.at[o, k], li_in.at[near, k], cond)
        if o < C - 1:
            copy(lig.at[near, k], lig.at[near, k], li_r.at[o, k], li_in.at[near, k],
                 (r, c + 1, d), jnp.logical_and(cond, c < C - 1))

    half = (K + 1) // 2
    for k in range(half):
        send_li(k)
        send_ri(k)

    for k in range(K):
        tp[k] = mm(lo[k], ct[...], (0, 0))
    for o in range(1, C):
        n = col_peer(o)
        copy(tp.at[pl.ds(n * KC, KC)], tpr.at[c], tp_s.at[o], tp_in.at[c], (r, n, d))
    for k in range(K):
        pp[k] = mm(rt[...], ro[k], (0, 0))
    for o in range(1, R):
        n = row_peer(o)
        copy(pp.at[pl.ds(n * KR, KR)], ppr.at[r], pp_s.at[o], pp_in.at[r], (n, c, d))
    for k in range(half, K):
        send_li(k)
        send_ri(k)
    lig[c] = li[...]
    rig[r] = ri[...]

    for k in range(K):
        forward_li(1, k)

    total = tp[pl.ds(c * KC, KC)]
    for o in range(1, C):
        n = col_peer(o)
        arrive(tpr.at[n], tp_s.at[o], tp_in.at[n])
        total = total + tpr[n]
    test[c] = total.astype(BF16)
    for o in range(1, C):
        copy(test.at[c], test.at[c], te_s.at[o], te_in.at[c], (r, col_peer(o), d))
    total = pp[pl.ds(r * KR, KR)]
    for o in range(1, R):
        n = row_peer(o)
        arrive(ppr.at[n], pp_s.at[o], pp_in.at[n])
        total = total + ppr[n]
    probe[r] = total.astype(BF16)
    for o in range(1, R):
        copy(probe.at[r], probe.at[r], pr_s.at[o], pr_in.at[r], (row_peer(o), c, d))

    for o in range(2, C - 1):
        for k in range(K):
            forward_li(o, k)

    for k in range(K):
        for o in range(1, R):
            n = row_peer(o)
            arrive(rig.at[n, k], ri_s.at[o, k], ri_in.at[n, k])
    for o in range(1, R):
        n = row_peer(o)
        arrive(probe.at[n], pr_s.at[o], pr_in.at[n])
    for o in range(1, C):
        n = col_peer(o)
        arrive(test.at[n], te_s.at[o], te_in.at[n])

    scale = (K * D) ** -0.5
    core_left = []
    core_part = None
    for k in range(K):
        if C > 2:
            forward_li(C - 1, k)
        cross = None
        for b in range(C):
            term = mm(rig[b, k], lig[b, k], (0, 0))
            cross = term if cross is None else cross + term
        cross = cross.astype(BF16)
        weight = mask[0, 0, k].astype(F32) * scale
        right = (mm(probe[k // KR, k % KR], cross) * weight).astype(BF16)
        crt[c, k] = right
        for o in range(1, C):
            copy(crt.at[c, k], crt.at[c, k], cr_s.at[o, k], cr_in.at[c, k], (r, col_peer(o), d))
        test_k = test[k // KC, k % KC]
        core_left.append((mm(cross, test_k) * weight).astype(BF16))
        term = mm(right, test_k)
        core_part = term if core_part is None else core_part + term

    cps[...] = core_part
    for o in range(1, D):
        copy(cps, cpr.at[d], cp_s.at[o], cp_in.at[d], (r, c, depth_peer(o)))
    cpr[d] = core_part
    for o in range(1, D):
        n = depth_peer(o)
        arrive(cpr.at[n], cp_s.at[o], cp_in.at[n])
    core = cpr[0]
    for n in range(1, D):
        core = core + cpr[n]

    gram = mm(core, core, (1, 1), HIGHEST)
    eye = (
        lax.broadcasted_iota(jnp.int32, (rank, rank), 0)
        == lax.broadcasted_iota(jnp.int32, (rank, rank), 1)
    ).astype(F32)
    trace = jnp.sum(gram * eye)
    ridge = 0.05 * trace / rank + 1e-05
    gram = gram + ridge * eye
    start, scales = inverse_schedule(rank)
    first = start / jnp.broadcast_to(trace + ridge, (rank, rank))
    inv = (scales[0] * first) * (2.0 * eye - first * gram)
    for factor in scales[1:]:
        step = 2.0 * eye - mm(gram, inv, precision=HIGHEST)
        inv = factor * mm(inv, step, precision=HIGHEST)
    weights = (mm(inv, core, precision=HIGHEST) * rank**0.5).astype(BF16)

    for k in range(K):
        zz[r, k] = mm(core_left[k], weights, (1, 1)).astype(BF16)
    for o in range(1, R):
        copy(zz.at[r], zz.at[r], z_s.at[o], z_in.at[r], (row_peer(o), c, d))

    part_l = lo.shape[1] // D
    for o in range(C):
        j = col_peer(o)
        if o > 0:
            for k in range(K):
                arrive(crt.at[j, k], cr_s.at[o, k], cr_in.at[j, k])
        total = None
        for k in range(K):
            term = mm(lo[k], crt[j, k], (1, 1))
            total = term if total is None else total + term
        for n in range(D):
            rps[n, j] = total[n * part_l:(n + 1) * part_l]
    for o in range(1, D):
        n = depth_peer(o)
        copy(rps.at[n], rpr.at[d], rp_s.at[o], rp_in.at[d], (r, c, n))
    total = rps[d]
    for o in range(1, D):
        n = depth_peer(o)
        arrive(rpr.at[n], rp_s.at[o], rp_in.at[n])
        total = total + rpr[n]
    rsend[...] = total.astype(BF16)
    place = c * D + d
    owner, slot = place // C, lax.rem(place, C)
    for o in range(1, C):
        j = col_peer(o)
        copy(rsend.at[j], rout.at[slot], ro_s.at[o], ro_in.at[slot], (r, j, owner))
    copy(rsend.at[c], rout.at[slot], ro_s.at[0], ro_in.at[slot], (r, c, owner), owner != d)

    part_r = ro.shape[1] // D
    for o in range(R):
        i = row_peer(o)
        if o > 0:
            arrive(zz.at[i], z_s.at[o], z_in.at[i])
        total = None
        for k in range(K):
            term = mm(ro[k], zz[i, k])
            total = term if total is None else total + term
        for n in range(D):
            qps[n, i] = total[n * part_r:(n + 1) * part_r]
    for o in range(1, D):
        n = depth_peer(o)
        copy(qps.at[n], qpr.at[d], qp_s.at[o], qp_in.at[d], (r, c, n))
    total = qps[d]
    for o in range(1, D):
        n = depth_peer(o)
        arrive(qpr.at[n], qp_s.at[o], qp_in.at[n])
        total = total + qpr[n]
    qsend[...] = total.astype(BF16)
    place_q = r * D + d
    owner_q, slot_q = place_q // R, lax.rem(place_q, R)
    for o in range(1, R):
        i = row_peer(o)
        copy(qsend.at[i], qout.at[slot_q], qo_s.at[o], qo_in.at[slot_q], (i, c, owner_q))
    copy(qsend.at[r], qout.at[slot_q], qo_s.at[0], qo_in.at[slot_q], (r, c, owner_q), owner_q != d)

    @pl.when(owner == d)
    def _():
        rout[slot] = rsend[c]

    @pl.when(owner_q == d)
    def _():
        qout[slot_q] = qsend[r]

    for q in range(C):
        src = d * C + q
        mine = jnp.logical_and(src // D == c, lax.rem(src, D) == d)
        arrive(rout.at[q], ro_s.at[0], ro_in.at[q], jnp.logical_not(mine))
        out_range[q * part_l:(q + 1) * part_l, :] = rout[q].astype(F32)
    for q in range(R):
        src = d * R + q
        mine = jnp.logical_and(src // D == r, lax.rem(src, D) == d)
        arrive(qout.at[q], qo_s.at[0], qo_in.at[q], jnp.logical_not(mine))
        out_corange[q * part_r:(q + 1) * part_r, :] = qout[q].astype(F32)
    for cond, op in pending:
        guarded(cond, op.wait_send)


def body(sizes, left_outer, left_inner, right_outer, right_inner, range_test, corange_test, product_mask):
    R, C, D = sizes
    K, BL, rank = left_outer.shape[1:]
    BR = right_outer.shape[2]
    sketch = corange_test.shape[2]
    assert R == C and K % R == 0 and BL % D == 0
    KR, KC = K // R, K // C
    dma = pltpu.SemaphoreType.DMA
    vmem = pltpu.VMEM
    scratch = [
        vmem((C, K, BL, rank), BF16),
        vmem((R, K, BR, rank), BF16),
        vmem((K, rank, rank), F32),
        vmem((R, KR, rank, rank), F32),
        vmem((R, KR, rank, rank), BF16),
        vmem((K, rank, sketch), F32),
        vmem((C, KC, rank, sketch), F32),
        vmem((C, KC, rank, sketch), BF16),
        vmem((C, K, rank, rank), BF16),
        vmem((rank, sketch), F32),
        vmem((D, rank, sketch), F32),
        vmem((R, K, rank, rank), BF16),
        vmem((D, C, BL // D, rank), F32),
        vmem((D, C, BL // D, rank), F32),
        vmem((C, BL // D, rank), BF16),
        vmem((C, BL // D, rank), BF16),
        vmem((D, R, BR // D, rank), F32),
        vmem((D, R, BR // D, rank), F32),
        vmem((R, BR // D, rank), BF16),
        vmem((R, BR // D, rank), BF16),
        dma((C, K)), dma((C, K)), dma((C, K)), dma((R, K)), dma((R, K)),
        dma((R,)), dma((R,)), dma((R,)), dma((R,)),
        dma((C,)), dma((C,)), dma((C,)), dma((C,)),
        dma((C, K)), dma((C, K)), dma((D,)), dma((D,)), dma((R,)), dma((R,)),
        dma((D,)), dma((D,)), dma((C,)), dma((C,)),
        dma((D,)), dma((D,)), dma((R,)), dma((R,)),
    ]
    tile = BL * C
    whole = pl.BlockSpec(memory_space=pltpu.VMEM)
    out = jax.ShapeDtypeStruct((tile // D, rank), F32)
    range_rows, corange_rows = pl.pallas_call(
        functools.partial(kernel, (R, C, D, K)),
        out_shape=(out, out),
        in_specs=[whole] * 6 + [pl.BlockSpec(memory_space=pltpu.SMEM)],
        out_specs=(whole, whole),
        scratch_shapes=scratch,
        compiler_params=pltpu.CompilerParams(
            collective_id=0, has_side_effects=True, vmem_limit_bytes=60 * 1024 * 1024
        ),
    )(left_outer[0], left_inner[0], right_outer[0], right_inner[0],
      range_test[0], corange_test[0], product_mask)
    return range_rows[None, None], corange_rows[None, None]


def solution(mesh):
    sizes = tuple(mesh.shape[name] for name in ("row", "col", "depth"))
    return jax.shard_map(
        functools.partial(body, sizes),
        mesh=mesh,
        in_specs=(
            P("row", "depth", "col", None),
            P("row", "depth", "col", None),
            P("col", "depth", "row", None),
            P("col", "depth", "row", None),
            P("col", "row", None),
            P("row", "col", None),
            P("row", "col", "depth"),
        ),
        out_specs=(P("row", "col", "depth", None), P("row", "col", "depth", None)),
        check_vma=False,
    )
```

```python
import functools

import jax
import jax.numpy as jnp
from jax import lax
from jax.experimental import pallas as pl
from jax.experimental.pallas import tpu as pltpu
from jax.sharding import PartitionSpec as P

F32 = jnp.float32
BF16 = jnp.bfloat16
HIGHEST = lax.Precision.HIGHEST
MESH = pl.DeviceIdType.MESH


def mm(a, b, contract=(1, 0), precision=None):
    dims = (((contract[0],), (contract[1],)), ((), ()))
    return lax.dot_general(a, b, dims, precision=precision, preferred_element_type=F32)


def guarded(cond, action):
    if cond is None:
        action()
    else:
        pl.when(cond)(action)


def inverse_schedule(rank):
    low = 1.0 / (rank / 0.05 + 1.0)
    low *= 0.999
    start = 2.0 / (1.0 + low)
    err = 1.0 - low * start
    scales = []
    while err > 1e-8:
        scales.append(2.0 / (2.0 - err * err))
        err = err * err / (2.0 - err * err)
    return start, scales


def kernel(
    sizes,
    lo, li, ro, ri, rt, ct, mask,
    out_range, out_corange,
    lig, rig, pp, ppr, probe, tp, tpr, test, crt, cps, cpr, zz,
    rps, rpr, rsend, rout, qps, qpr, qsend, qout,
    li_l, li_r, li_in, ri_s, ri_in,
    pp_s, pp_in, pr_s, pr_in, tp_s, tp_in, te_s, te_in,
    cr_s, cr_in, cp_s, cp_in, z_s, z_in,
    rp_s, rp_in, ro_s, ro_in, qp_s, qp_in, qo_s, qo_in,
):
    R, C, D, K = sizes
    KR, KC = K // R, K // C
    rank = lo.shape[2]
    r, c, d = lax.axis_index("row"), lax.axis_index("col"), lax.axis_index("depth")
    pending = []

    def copy(src, dst, send, recv, dev, cond=None):
        op = pltpu.make_async_remote_copy(
            src_ref=src, dst_ref=dst, send_sem=send, recv_sem=recv,
            device_id=dev, device_id_type=MESH,
        )
        guarded(cond, op.start)
        pending.append((cond, op))

    def arrive(dst, send, recv, cond=None):
        op = pltpu.make_async_remote_copy(
            src_ref=dst, dst_ref=dst, send_sem=send, recv_sem=recv,
            device_id=(r, c, d), device_id_type=MESH,
        )
        guarded(cond, op.wait_recv)

    def row_peer(o):
        return lax.rem(r + o, R)

    def col_peer(o):
        return lax.rem(c + o, C)

    def depth_peer(o):
        return lax.rem(d + o, D)

    bar = pltpu.get_barrier_semaphore()

    @pl.loop(1, R * D)
    def _(o):
        n = lax.rem(r * D + d + o, R * D)
        pl.semaphore_signal(bar, inc=1, device_id=(n // D, c, lax.rem(n, D)), device_id_type=MESH)

    @pl.loop(1, C * D)
    def _(o):
        n = lax.rem(c * D + d + o, C * D)
        pl.semaphore_signal(bar, inc=1, device_id=(r, n // D, lax.rem(n, D)), device_id_type=MESH)

    pl.semaphore_wait(bar, R * D + C * D - 2)

    def send_li(k):
        copy(li.at[k], lig.at[c, k], li_l.at[0, k], li_in.at[c, k], (r, c - 1, d), c > 0)
        copy(li.at[k], lig.at[c, k], li_r.at[0, k], li_in.at[c, k], (r, c + 1, d), c < C - 1)

    def send_ri(k):
        for o in range(1, R):
            copy(rig.at[r, k], rig.at[r, k], ri_s.at[o, k], ri_in.at[r, k], (row_peer(o), c, d))

    def forward_li(o, k):
        far = c + o
        cond = far < C
        arrive(lig.at[far, k], li_l.at[o, k], li_in.at[far, k], cond)
        if o < C - 1:
            copy(lig.at[far, k], lig.at[far, k], li_l.at[o, k], li_in.at[far, k],
                 (r, c - 1, d), jnp.logical_and(cond, c > 0))
        near = c - o
        cond = near >= 0
        arrive(lig.at[near, k], li_r.at[o, k], li_in.at[near, k], cond)
        if o < C - 1:
            copy(lig.at[near, k], lig.at[near, k], li_r.at[o, k], li_in.at[near, k],
                 (r, c + 1, d), jnp.logical_and(cond, c < C - 1))

    half = (K + 1) // 2
    for k in range(half):
        send_li(k)
    for k in range(half):
        rig[r, k] = ri[k].T
        send_ri(k)

    ct_rows = ct[...].T
    for k in range(K):
        tp[k] = mm(ct_rows, lo[k])
    for o in range(1, C):
        n = col_peer(o)
        copy(tp.at[pl.ds(n * KC, KC)], tpr.at[c], tp_s.at[o], tp_in.at[c], (r, n, d))
    rt_rows = rt[...].T
    for k in range(K):
        pp[k] = mm(rt_rows, ro[k])
    for o in range(1, R):
        n = row_peer(o)
        copy(pp.at[pl.ds(n * KR, KR)], ppr.at[r], pp_s.at[o], pp_in.at[r], (n, c, d))
    for k in range(half, K):
        send_li(k)
    for k in range(half, K):
        rig[r, k] = ri[k].T
        send_ri(k)
    lig[c] = li[...]

    for k in range(K):
        forward_li(1, k)

    total = tp[pl.ds(c * KC, KC)]
    for o in range(1, C):
        n = col_peer(o)
        arrive(tpr.at[n], tp_s.at[o], tp_in.at[n])
        total = total + tpr[n]
    test[c] = total.astype(BF16)
    for o in range(1, C):
        copy(test.at[c], test.at[c], te_s.at[o], te_in.at[c], (r, col_peer(o), d))
    total = pp[pl.ds(r * KR, KR)]
    for o in range(1, R):
        n = row_peer(o)
        arrive(ppr.at[n], pp_s.at[o], pp_in.at[n])
        total = total + ppr[n]
    probe[r] = total.astype(BF16)
    for o in range(1, R):
        copy(probe.at[r], probe.at[r], pr_s.at[o], pr_in.at[r], (row_peer(o), c, d))

    for o in range(2, C - 1):
        for k in range(K):
            forward_li(o, k)

    for k in range(K):
        for o in range(1, R):
            n = row_peer(o)
            arrive(rig.at[n, k], ri_s.at[o, k], ri_in.at[n, k])
    for o in range(1, R):
        n = row_peer(o)
        arrive(probe.at[n], pr_s.at[o], pr_in.at[n])
    for o in range(1, C):
        n = col_peer(o)
        arrive(test.at[n], te_s.at[o], te_in.at[n])

    scale = (K * D) ** -0.5
    core_left = []
    core_part = None
    for k in range(K):
        if C > 2:
            forward_li(C - 1, k)
        cross = None
        for b in range(C):
            term = mm(rig[b, k], lig[b, k])
            cross = term if cross is None else cross + term
        cross = cross.astype(BF16)
        weight = mask[0, 0, k].astype(F32) * scale
        right = (mm(probe[k // KR, k % KR], cross) * weight).astype(BF16)
        lanes = pl.ds(k * rank, rank)
        crt[c, :, lanes] = right
        for o in range(1, C):
            copy(crt.at[c, :, lanes], crt.at[c, :, lanes], cr_s.at[o, k], cr_in.at[c, k],
                 (r, col_peer(o), d))
        test_k = test[k // KC, k % KC]
        core_left.append((mm(cross, test_k, (1, 1)) * weight).astype(BF16))
        term = mm(right, test_k, (1, 1))
        core_part = term if core_part is None else core_part + term

    cps[...] = core_part
    for o in range(1, D):
        copy(cps, cpr.at[d], cp_s.at[o], cp_in.at[d], (r, c, depth_peer(o)))
    cpr[d] = core_part
    for o in range(1, D):
        n = depth_peer(o)
        arrive(cpr.at[n], cp_s.at[o], cp_in.at[n])
    core = cpr[0]
    for n in range(1, D):
        core = core + cpr[n]

    gram = mm(core, core, (1, 1), HIGHEST)
    eye = (
        lax.broadcasted_iota(jnp.int32, (rank, rank), 0)
        == lax.broadcasted_iota(jnp.int32, (rank, rank), 1)
    ).astype(F32)
    trace = jnp.sum(gram * eye)
    ridge = 0.05 * trace / rank + 1e-05
    gram = gram + ridge * eye
    start, scales = inverse_schedule(rank)
    first = start / jnp.broadcast_to(trace + ridge, (rank, rank))
    inv = (scales[0] * first) * (2.0 * eye - first * gram)
    for factor in scales[1:]:
        step = 2.0 * eye - mm(gram, inv, precision=HIGHEST)
        inv = factor * mm(inv, step, precision=HIGHEST)
    weights = (mm(inv, core, precision=HIGHEST) * rank**0.5).astype(BF16)

    for k in range(K):
        rows = pl.ds(k * rank, rank)
        zz[r, rows] = mm(core_left[k], weights, (1, 1)).astype(BF16)
        for o in range(1, R):
            copy(zz.at[r, rows], zz.at[r, rows], z_s.at[o, k], z_in.at[r, k], (row_peer(o), c, d))

    part_l = lo.shape[1] // D
    place = c * D + d
    owner, slot = place // C, lax.rem(place, C)
    lo_all = jnp.concatenate([lo[k] for k in range(K)], axis=1)
    for o in range(C):
        j = col_peer(o)
        if o > 0:
            for k in range(K):
                lanes = pl.ds(k * rank, rank)
                arrive(crt.at[j, :, lanes], cr_s.at[o, k], cr_in.at[j, k])
        total = mm(lo_all, crt[j], (1, 1))
        for n in range(D):
            rps[n, j] = total[n * part_l:(n + 1) * part_l]
        for e in range(1, D):
            n = depth_peer(e)
            copy(rps.at[n, j], rpr.at[d, j], rp_s.at[e, o], rp_in.at[d, j], (r, c, n))
    for o in range(C):
        j = col_peer(o)
        total = rps[d, j]
        for e in range(1, D):
            n = depth_peer(e)
            arrive(rpr.at[n, j], rp_s.at[e, o], rp_in.at[n, j])
            total = total + rpr[n, j]
        rsend[j] = total.astype(BF16)
        copy(rsend.at[j], rout.at[slot], ro_s.at[o], ro_in.at[slot], (r, j, owner),
             owner != d if o == 0 else None)

    part_r = ro.shape[1] // D
    place_q = r * D + d
    owner_q, slot_q = place_q // R, lax.rem(place_q, R)
    ro_all = jnp.concatenate([ro[k] for k in range(K)], axis=1)
    for o in range(R):
        i = row_peer(o)
        if o > 0:
            for k in range(K):
                rows = pl.ds(k * rank, rank)
                arrive(zz.at[i, rows], z_s.at[o, k], z_in.at[i, k])
        total = mm(ro_all, zz[i])
        for n in range(D):
            qps[n, i] = total[n * part_r:(n + 1) * part_r]
        for e in range(1, D):
            n = depth_peer(e)
            copy(qps.at[n, i], qpr.at[d, i], qp_s.at[e, o], qp_in.at[d, i], (r, c, n))
    for o in range(R):
        i = row_peer(o)
        total = qps[d, i]
        for e in range(1, D):
            n = depth_peer(e)
            arrive(qpr.at[n, i], qp_s.at[e, o], qp_in.at[n, i])
            total = total + qpr[n, i]
        qsend[i] = total.astype(BF16)
        copy(qsend.at[i], qout.at[slot_q], qo_s.at[o], qo_in.at[slot_q], (i, c, owner_q),
             owner_q != d if o == 0 else None)

    @pl.when(owner == d)
    def _():
        rout[slot] = rsend[c]

    @pl.when(owner_q == d)
    def _():
        qout[slot_q] = qsend[r]

    for q in range(C):
        src = d * C + q
        mine = jnp.logical_and(src // D == c, lax.rem(src, D) == d)
        arrive(rout.at[q], ro_s.at[0], ro_in.at[q], jnp.logical_not(mine))
        out_range[q * part_l:(q + 1) * part_l, :] = rout[q]
    for q in range(R):
        src = d * R + q
        mine = jnp.logical_and(src // D == r, lax.rem(src, D) == d)
        arrive(qout.at[q], qo_s.at[0], qo_in.at[q], jnp.logical_not(mine))
        out_corange[q * part_r:(q + 1) * part_r, :] = qout[q]
    for cond, op in pending:
        guarded(cond, op.wait_send)


def body(sizes, left_outer, left_inner, right_outer, right_inner, range_test, corange_test, product_mask):
    R, C, D = sizes
    K, BL, rank = left_outer.shape[1:]
    BR = right_outer.shape[2]
    sketch = corange_test.shape[2]
    assert R == C and K % R == 0 and BL % D == 0
    KR, KC = K // R, K // C
    dma = pltpu.SemaphoreType.DMA
    vmem = pltpu.VMEM
    scratch = [
        vmem((C, K, BL, rank), BF16),
        vmem((R, K, rank, BR), BF16),
        vmem((K, rank, rank), F32),
        vmem((R, KR, rank, rank), F32),
        vmem((R, KR, rank, rank), BF16),
        vmem((K, sketch, rank), F32),
        vmem((C, KC, sketch, rank), F32),
        vmem((C, KC, sketch, rank), BF16),
        vmem((C, rank, K * rank), BF16),
        vmem((rank, sketch), F32),
        vmem((D, rank, sketch), F32),
        vmem((R, K * rank, rank), BF16),
        vmem((D, C, BL // D, rank), F32),
        vmem((D, C, BL // D, rank), F32),
        vmem((C, BL // D, rank), BF16),
        vmem((C, BL // D, rank), BF16),
        vmem((D, R, BR // D, rank), F32),
        vmem((D, R, BR // D, rank), F32),
        vmem((R, BR // D, rank), BF16),
        vmem((R, BR // D, rank), BF16),
        dma((C, K)), dma((C, K)), dma((C, K)), dma((R, K)), dma((R, K)),
        dma((R,)), dma((R,)), dma((R,)), dma((R,)),
        dma((C,)), dma((C,)), dma((C,)), dma((C,)),
        dma((C, K)), dma((C, K)), dma((D,)), dma((D,)), dma((R, K)), dma((R, K)),
        dma((D, C)), dma((D, C)), dma((C,)), dma((C,)),
        dma((D, R)), dma((D, R)), dma((R,)), dma((R,)),
    ]
    tile = BL * C
    whole = pl.BlockSpec(memory_space=pltpu.VMEM)
    out = jax.ShapeDtypeStruct((tile // D, rank), BF16)
    range_rows, corange_rows = pl.pallas_call(
        functools.partial(kernel, (R, C, D, K)),
        out_shape=(out, out),
        in_specs=[whole] * 6 + [pl.BlockSpec(memory_space=pltpu.SMEM)],
        out_specs=(whole, whole),
        scratch_shapes=scratch,
        compiler_params=pltpu.CompilerParams(
            collective_id=0, has_side_effects=True, vmem_limit_bytes=60 * 1024 * 1024
        ),
    )(left_outer[0], left_inner[0], right_outer[0], right_inner[0],
      range_test[0], corange_test[0], product_mask)
    return range_rows[None, None].astype(F32), corange_rows[None, None].astype(F32)


def solution(mesh):
    sizes = tuple(mesh.shape[name] for name in ("row", "col", "depth"))
    return jax.shard_map(
        functools.partial(body, sizes),
        mesh=mesh,
        in_specs=(
            P("row", "depth", "col", None),
            P("row", "depth", "col", None),
            P("col", "depth", "row", None),
            P("col", "depth", "row", None),
            P("col", "row", None),
            P("row", "col", None),
            P("row", "col", "depth"),
        ),
        out_specs=(P("row", "col", "depth", None), P("row", "col", "depth", None)),
        check_vma=False,
    )
```

```python
import functools

import jax
import jax.numpy as jnp
from jax import lax
from jax.experimental import pallas as pl
from jax.experimental.pallas import tpu as pltpu
from jax.sharding import PartitionSpec as P

F32 = jnp.float32
BF16 = jnp.bfloat16
HIGHEST = lax.Precision.HIGHEST
MESH = pl.DeviceIdType.MESH


def mm(a, b, contract=(1, 0), precision=None):
    dims = (((contract[0],), (contract[1],)), ((), ()))
    return lax.dot_general(a, b, dims, precision=precision, preferred_element_type=F32)


def guarded(cond, action):
    if cond is None:
        action()
    else:
        pl.when(cond)(action)


def inverse_schedule(rank):
    low = 1.0 / (rank / 0.05 + 1.0)
    low *= 0.999
    start = 2.0 / (1.0 + low)
    err = 1.0 - low * start
    scales = []
    while err > 1e-8:
        scales.append(2.0 / (2.0 - err * err))
        err = err * err / (2.0 - err * err)
    return start, scales


def kernel(
    sizes,
    lo, li, ro, ri, rt, ct, mask,
    out_range, out_corange,
    lig, rig, pp, ppr, probe, tp, tpr, test, crt, cps, cpr, zz,
    rps, rpr, rsend, rout, qps, qpr, qsend, qout, ext, xs, xr, cx,
    li_l, li_r, li_in, ri_s, ri_in,
    pp_s, pp_in, pr_s, pr_in, tp_s, tp_in, te_s, te_in,
    cr_s, cr_in, cp_s, cp_in, z_s, z_in,
    rp_s, rp_in, ro_s, ro_in, qp_s, qp_in, qo_s, qo_in, ext_s, ext_in, x_s,
):
    R, C, D, K = sizes
    KR, KC = K // R, K // C
    rank = lo.shape[2]
    r, c, d = lax.axis_index("row"), lax.axis_index("col"), lax.axis_index("depth")
    pending = []

    def copy(src, dst, send, recv, dev, cond=None):
        op = pltpu.make_async_remote_copy(
            src_ref=src, dst_ref=dst, send_sem=send, recv_sem=recv,
            device_id=dev, device_id_type=MESH,
        )
        guarded(cond, op.start)
        pending.append((cond, op))

    def arrive(dst, send, recv, cond=None):
        op = pltpu.make_async_remote_copy(
            src_ref=dst, dst_ref=dst, send_sem=send, recv_sem=recv,
            device_id=(r, c, d), device_id_type=MESH,
        )
        guarded(cond, op.wait_recv)

    def row_peer(o):
        return lax.rem(r + o, R)

    def col_peer(o):
        return lax.rem(c + o, C)

    def depth_peer(o):
        return lax.rem(d + o, D)

    bar = pltpu.get_barrier_semaphore()

    @pl.loop(1, R * D)
    def _(o):
        n = lax.rem(r * D + d + o, R * D)
        pl.semaphore_signal(bar, inc=1, device_id=(n // D, c, lax.rem(n, D)), device_id_type=MESH)

    @pl.loop(1, C * D)
    def _(o):
        n = lax.rem(c * D + d + o, C * D)
        pl.semaphore_signal(bar, inc=1, device_id=(r, n // D, lax.rem(n, D)), device_id_type=MESH)

    pl.semaphore_wait(bar, R * D + C * D - 2)

    moved = K - 1 if C >= 4 else K
    at_end = jnp.logical_or(c == 0, c == C - 1)
    inside = jnp.logical_and(c > 0, c < C - 1)
    helper = jnp.logical_or(c == 1, c == C - 2)
    near_end = 1 + (c // (C - 1)) * (C - 3)
    served = ((c - 1) // max(C - 3, 1)) * (C - 1)

    def send_li(k):
        skip = 1 if k == moved else 0
        copy(li.at[k], lig.at[c, k], li_l.at[0, k], li_in.at[c, k], (r, c - 1, d), c > skip)
        copy(li.at[k], lig.at[c, k], li_r.at[0, k], li_in.at[c, k], (r, c + 1, d), c < C - 1 - skip)

    def send_ri(k):
        if k == moved:
            copy(rig.at[r, k], ext.at[r], ext_s.at[0], ext_in.at[r], (r, near_end, d), at_end)
        for o in range(1, R):
            copy(rig.at[r, k], rig.at[r, k], ri_s.at[o, k], ri_in.at[r, k], (row_peer(o), c, d),
                 inside if k == moved else None)

    def forward_li(o, k):
        skip = 1 if k == moved else 0
        far = c + o
        cond = jnp.logical_and(far < C, c >= skip)
        arrive(lig.at[far, k], li_l.at[o, k], li_in.at[far, k], cond)
        if o < C - 1:
            copy(lig.at[far, k], lig.at[far, k], li_l.at[o, k], li_in.at[far, k],
                 (r, c - 1, d), jnp.logical_and(cond, c > skip))
        near = c - o
        cond = jnp.logical_and(near >= 0, c < C - skip)
        arrive(lig.at[near, k], li_r.at[o, k], li_in.at[near, k], cond)
        if o < C - 1:
            copy(lig.at[near, k], lig.at[near, k], li_r.at[o, k], li_in.at[near, k],
                 (r, c + 1, d), jnp.logical_and(cond, c < C - 1 - skip))

    half = (K + 1) // 2
    for k in range(half):
        send_li(k)
    for k in range(half):
        rig[r, k] = ri[k].T
        send_ri(k)

    ct_rows = ct[...].T
    for k in range(K):
        tp[k] = mm(ct_rows, lo[k])
    for o in range(1, C):
        n = col_peer(o)
        copy(tp.at[pl.ds(n * KC, KC)], tpr.at[c], tp_s.at[o], tp_in.at[c], (r, n, d))
    rt_rows = rt[...].T
    for k in range(K):
        pp[k] = mm(rt_rows, ro[k])
    for o in range(1, R):
        n = row_peer(o)
        copy(pp.at[pl.ds(n * KR, KR)], ppr.at[r], pp_s.at[o], pp_in.at[r], (n, c, d))
    for k in range(half, K):
        send_li(k)
    for k in range(half, K):
        rig[r, k] = ri[k].T
        send_ri(k)
    lig[c] = li[...]

    for k in range(K):
        forward_li(1, k)

    if moved < K:
        arrive(ext.at[r], ext_s.at[0], ext_in.at[r], helper)
        for o in range(1, R):
            copy(ext.at[r], ext.at[r], ext_s.at[o], ext_in.at[r], (row_peer(o), c, d), helper)

    total = tp[pl.ds(c * KC, KC)]
    for o in range(1, C):
        n = col_peer(o)
        arrive(tpr.at[n], tp_s.at[o], tp_in.at[n])
        total = total + tpr[n]
    test[c] = total.astype(BF16)
    for o in range(1, C):
        copy(test.at[c], test.at[c], te_s.at[o], te_in.at[c], (r, col_peer(o), d))
    total = pp[pl.ds(r * KR, KR)]
    for o in range(1, R):
        n = row_peer(o)
        arrive(ppr.at[n], pp_s.at[o], pp_in.at[n])
        total = total + ppr[n]
    probe[r] = total.astype(BF16)
    for o in range(1, R):
        copy(probe.at[r], probe.at[r], pr_s.at[o], pr_in.at[r], (row_peer(o), c, d))

    for o in range(2, C - 1):
        for k in range(K):
            forward_li(o, k)

    for k in range(K):
        for o in range(1, R):
            n = row_peer(o)
            arrive(rig.at[n, k], ri_s.at[o, k], ri_in.at[n, k], inside if k == moved else None)

    def cross_of(block, k):
        total = None
        for b in range(C):
            term = mm(block(b), lig[b, k])
            total = term if total is None else total + term
        return total.astype(BF16)

    if moved < K:
        for o in range(1, R):
            n = row_peer(o)
            arrive(ext.at[n], ext_s.at[o], ext_in.at[n], helper)

        @pl.when(helper)
        def _():
            xs[...] = cross_of(lambda b: ext[b], moved)

        copy(xs, xr, x_s.at[0], x_s.at[1], (r, served, d), helper)

        @pl.when(inside)
        def _():
            cx[...] = cross_of(lambda b: rig[b, moved], moved)

    for o in range(1, R):
        n = row_peer(o)
        arrive(probe.at[n], pr_s.at[o], pr_in.at[n])
    for o in range(1, C):
        n = col_peer(o)
        arrive(test.at[n], te_s.at[o], te_in.at[n])

    scale = (K * D) ** -0.5
    core_left = []
    core_part = None
    for k in range(K):
        if C > 2:
            forward_li(C - 1, k)
        if k == moved:
            arrive(xr, x_s.at[0], x_s.at[1], at_end)

            @pl.when(at_end)
            def _():
                cx[...] = xr[...]

            cross = cx[...]
        else:
            cross = cross_of(lambda b: rig[b, k], k)
        weight = mask[0, 0, k].astype(F32) * scale
        right = (mm(probe[k // KR, k % KR], cross) * weight).astype(BF16)
        lanes = pl.ds(k * rank, rank)
        crt[c, :, lanes] = right
        for o in range(1, C):
            copy(crt.at[c, :, lanes], crt.at[c, :, lanes], cr_s.at[o, k], cr_in.at[c, k],
                 (r, col_peer(o), d))
        test_k = test[k // KC, k % KC]
        core_left.append((mm(cross, test_k, (1, 1)) * weight).astype(BF16))
        term = mm(right, test_k, (1, 1))
        core_part = term if core_part is None else core_part + term

    cps[...] = core_part
    for o in range(1, D):
        copy(cps, cpr.at[d], cp_s.at[o], cp_in.at[d], (r, c, depth_peer(o)))
    cpr[d] = core_part
    for o in range(1, D):
        n = depth_peer(o)
        arrive(cpr.at[n], cp_s.at[o], cp_in.at[n])
    core = cpr[0]
    for n in range(1, D):
        core = core + cpr[n]

    gram = mm(core, core, (1, 1), HIGHEST)
    eye = (
        lax.broadcasted_iota(jnp.int32, (rank, rank), 0)
        == lax.broadcasted_iota(jnp.int32, (rank, rank), 1)
    ).astype(F32)
    trace = jnp.sum(gram * eye)
    ridge = 0.05 * trace / rank + 1e-05
    gram = gram + ridge * eye
    start, scales = inverse_schedule(rank)
    first = start / jnp.broadcast_to(trace + ridge, (rank, rank))
    inv = (scales[0] * first) * (2.0 * eye - first * gram)
    for factor in scales[1:]:
        step = 2.0 * eye - mm(gram, inv, precision=HIGHEST)
        inv = factor * mm(inv, step, precision=HIGHEST)
    weights = (mm(inv, core, precision=HIGHEST) * rank**0.5).astype(BF16)

    for k in range(K):
        rows = pl.ds(k * rank, rank)
        zz[r, rows] = mm(core_left[k], weights, (1, 1)).astype(BF16)
        for o in range(1, R):
            copy(zz.at[r, rows], zz.at[r, rows], z_s.at[o, k], z_in.at[r, k], (row_peer(o), c, d))

    part_l = lo.shape[1] // D
    place = c * D + d
    owner, slot = place // C, lax.rem(place, C)
    lo_all = jnp.concatenate([lo[k] for k in range(K)], axis=1)
    for o in range(C):
        j = col_peer(o)
        if o > 0:
            for k in range(K):
                lanes = pl.ds(k * rank, rank)
                arrive(crt.at[j, :, lanes], cr_s.at[o, k], cr_in.at[j, k])
        total = mm(lo_all, crt[j], (1, 1))
        for n in range(D):
            rps[n, j] = total[n * part_l:(n + 1) * part_l]
        for e in range(1, D):
            n = depth_peer(e)
            copy(rps.at[n, j], rpr.at[d, j], rp_s.at[e, o], rp_in.at[d, j], (r, c, n))
    for o in range(C):
        j = col_peer(o)
        total = rps[d, j]
        for e in range(1, D):
            n = depth_peer(e)
            arrive(rpr.at[n, j], rp_s.at[e, o], rp_in.at[n, j])
            total = total + rpr[n, j]
        rsend[j] = total.astype(BF16)
        copy(rsend.at[j], rout.at[slot], ro_s.at[o], ro_in.at[slot], (r, j, owner),
             owner != d if o == 0 else None)

    part_r = ro.shape[1] // D
    place_q = r * D + d
    owner_q, slot_q = place_q // R, lax.rem(place_q, R)
    ro_all = jnp.concatenate([ro[k] for k in range(K)], axis=1)
    for o in range(R):
        i = row_peer(o)
        if o > 0:
            for k in range(K):
                rows = pl.ds(k * rank, rank)
                arrive(zz.at[i, rows], z_s.at[o, k], z_in.at[i, k])
        total = mm(ro_all, zz[i])
        for n in range(D):
            qps[n, i] = total[n * part_r:(n + 1) * part_r]
        for e in range(1, D):
            n = depth_peer(e)
            copy(qps.at[n, i], qpr.at[d, i], qp_s.at[e, o], qp_in.at[d, i], (r, c, n))
    for o in range(R):
        i = row_peer(o)
        total = qps[d, i]
        for e in range(1, D):
            n = depth_peer(e)
            arrive(qpr.at[n, i], qp_s.at[e, o], qp_in.at[n, i])
            total = total + qpr[n, i]
        qsend[i] = total.astype(BF16)
        copy(qsend.at[i], qout.at[slot_q], qo_s.at[o], qo_in.at[slot_q], (i, c, owner_q),
             owner_q != d if o == 0 else None)

    @pl.when(owner == d)
    def _():
        rout[slot] = rsend[c]

    @pl.when(owner_q == d)
    def _():
        qout[slot_q] = qsend[r]

    for q in range(C):
        src = d * C + q
        mine = jnp.logical_and(src // D == c, lax.rem(src, D) == d)
        arrive(rout.at[q], ro_s.at[0], ro_in.at[q], jnp.logical_not(mine))
        out_range[q * part_l:(q + 1) * part_l, :] = rout[q]
    for q in range(R):
        src = d * R + q
        mine = jnp.logical_and(src // D == r, lax.rem(src, D) == d)
        arrive(qout.at[q], qo_s.at[0], qo_in.at[q], jnp.logical_not(mine))
        out_corange[q * part_r:(q + 1) * part_r, :] = qout[q]
    for cond, op in pending:
        guarded(cond, op.wait_send)


def body(sizes, left_outer, left_inner, right_outer, right_inner, range_test, corange_test, product_mask):
    R, C, D = sizes
    K, BL, rank = left_outer.shape[1:]
    BR = right_outer.shape[2]
    sketch = corange_test.shape[2]
    assert R == C and K % R == 0 and BL % D == 0
    KR, KC = K // R, K // C
    dma = pltpu.SemaphoreType.DMA
    vmem = pltpu.VMEM
    scratch = [
        vmem((C, K, BL, rank), BF16),
        vmem((R, K, rank, BR), BF16),
        vmem((K, rank, rank), F32),
        vmem((R, KR, rank, rank), F32),
        vmem((R, KR, rank, rank), BF16),
        vmem((K, sketch, rank), F32),
        vmem((C, KC, sketch, rank), F32),
        vmem((C, KC, sketch, rank), BF16),
        vmem((C, rank, K * rank), BF16),
        vmem((rank, sketch), F32),
        vmem((D, rank, sketch), F32),
        vmem((R, K * rank, rank), BF16),
        vmem((D, C, BL // D, rank), F32),
        vmem((D, C, BL // D, rank), F32),
        vmem((C, BL // D, rank), BF16),
        vmem((C, BL // D, rank), BF16),
        vmem((D, R, BR // D, rank), F32),
        vmem((D, R, BR // D, rank), F32),
        vmem((R, BR // D, rank), BF16),
        vmem((R, BR // D, rank), BF16),
        vmem((R, rank, BR), BF16),
        vmem((rank, rank), BF16),
        vmem((rank, rank), BF16),
        vmem((rank, rank), BF16),
        dma((C, K)), dma((C, K)), dma((C, K)), dma((R, K)), dma((R, K)),
        dma((R,)), dma((R,)), dma((R,)), dma((R,)),
        dma((C,)), dma((C,)), dma((C,)), dma((C,)),
        dma((C, K)), dma((C, K)), dma((D,)), dma((D,)), dma((R, K)), dma((R, K)),
        dma((D, C)), dma((D, C)), dma((C,)), dma((C,)),
        dma((D, R)), dma((D, R)), dma((R,)), dma((R,)),
        dma((R,)), dma((R,)), dma((2,)),
    ]
    tile = BL * C
    whole = pl.BlockSpec(memory_space=pltpu.VMEM)
    out = jax.ShapeDtypeStruct((tile // D, rank), BF16)
    range_rows, corange_rows = pl.pallas_call(
        functools.partial(kernel, (R, C, D, K)),
        out_shape=(out, out),
        in_specs=[whole] * 6 + [pl.BlockSpec(memory_space=pltpu.SMEM)],
        out_specs=(whole, whole),
        scratch_shapes=scratch,
        compiler_params=pltpu.CompilerParams(
            collective_id=0, has_side_effects=True, vmem_limit_bytes=60 * 1024 * 1024
        ),
    )(left_outer[0], left_inner[0], right_outer[0], right_inner[0],
      range_test[0], corange_test[0], product_mask)
    return range_rows[None, None].astype(F32), corange_rows[None, None].astype(F32)


def solution(mesh):
    sizes = tuple(mesh.shape[name] for name in ("row", "col", "depth"))
    return jax.shard_map(
        functools.partial(body, sizes),
        mesh=mesh,
        in_specs=(
            P("row", "depth", "col", None),
            P("row", "depth", "col", None),
            P("col", "depth", "row", None),
            P("col", "depth", "row", None),
            P("col", "row", None),
            P("row", "col", None),
            P("row", "col", "depth"),
        ),
        out_specs=(P("row", "col", "depth", None), P("row", "col", "depth", None)),
        check_vma=False,
    )
```

```python
import functools

import jax
import jax.numpy as jnp
from jax import lax
from jax.experimental import pallas as pl
from jax.experimental.pallas import tpu as pltpu
from jax.sharding import PartitionSpec as P

F32 = jnp.float32
BF16 = jnp.bfloat16
HIGHEST = lax.Precision.HIGHEST
MESH = pl.DeviceIdType.MESH


def mm(a, b, contract=(1, 0), precision=None):
    dims = (((contract[0],), (contract[1],)), ((), ()))
    return lax.dot_general(a, b, dims, precision=precision, preferred_element_type=F32)


def guarded(cond, action):
    if cond is None:
        action()
    else:
        pl.when(cond)(action)


def inverse_schedule(rank):
    low = 1.0 / (rank / 0.05 + 1.0)
    low *= 0.999
    start = 2.0 / (1.0 + low)
    err = 1.0 - low * start
    scales = []
    while err > 1e-8:
        scales.append(2.0 / (2.0 - err * err))
        err = err * err / (2.0 - err * err)
    return start, scales


def kernel(
    sizes,
    lo, li, ro, ri, rt, ct, mask,
    out_range, out_corange,
    lig, rig, pp, ppr, probe, tp, tpr, test, crt, cps, cpr, zz,
    rps, rpr, rsend, rout, qps, qpr, qsend, qout, ext, xs, xr, cx,
    li_l, li_r, li_in, ri_s, ri_in,
    pp_s, pp_in, pr_s, pr_in, tp_s, tp_in, te_s, te_in,
    cr_s, cr_in, cp_s, cp_in, z_s, z_in,
    rp_s, rp_in, ro_s, ro_in, qp_s, qp_in, qo_s, qo_in, ext_s, ext_in, x_s,
):
    R, C, D, K = sizes
    KR, KC = K // R, K // C
    rank = lo.shape[2]
    r, c, d = lax.axis_index("row"), lax.axis_index("col"), lax.axis_index("depth")
    pending = []

    def copy(src, dst, send, recv, dev, cond=None):
        op = pltpu.make_async_remote_copy(
            src_ref=src, dst_ref=dst, send_sem=send, recv_sem=recv,
            device_id=dev, device_id_type=MESH,
        )
        guarded(cond, op.start)
        pending.append((cond, op))

    def arrive(dst, send, recv, cond=None):
        op = pltpu.make_async_remote_copy(
            src_ref=dst, dst_ref=dst, send_sem=send, recv_sem=recv,
            device_id=(r, c, d), device_id_type=MESH,
        )
        guarded(cond, op.wait_recv)

    def row_peer(o):
        return lax.rem(r + o, R)

    def col_peer(o):
        return lax.rem(c + o, C)

    def depth_peer(o):
        return lax.rem(d + o, D)

    bar = pltpu.get_barrier_semaphore()

    @pl.loop(1, R * D)
    def _(o):
        n = lax.rem(r * D + d + o, R * D)
        pl.semaphore_signal(bar, inc=1, device_id=(n // D, c, lax.rem(n, D)), device_id_type=MESH)

    @pl.loop(1, C * D)
    def _(o):
        n = lax.rem(c * D + d + o, C * D)
        pl.semaphore_signal(bar, inc=1, device_id=(r, n // D, lax.rem(n, D)), device_id_type=MESH)

    pl.semaphore_wait(bar, R * D + C * D - 2)

    moved = K - 1 if C >= 4 else K
    at_end = jnp.logical_or(c == 0, c == C - 1)
    inside = jnp.logical_and(c > 0, c < C - 1)
    helper = jnp.logical_or(c == 1, c == C - 2)
    near_end = 1 + (c // (C - 1)) * (C - 3)
    served = ((c - 1) // max(C - 3, 1)) * (C - 1)

    def send_li(k):
        skip = 1 if k == moved else 0
        copy(li.at[k], lig.at[c, k], li_l.at[0, k], li_in.at[c, k], (r, c - 1, d), c > skip)
        copy(li.at[k], lig.at[c, k], li_r.at[0, k], li_in.at[c, k], (r, c + 1, d), c < C - 1 - skip)

    def send_ri(k):
        if k == moved:
            copy(rig.at[r, k], ext.at[r], ext_s.at[0], ext_in.at[r], (r, near_end, d), at_end)
        for o in range(1, R):
            copy(rig.at[r, k], rig.at[r, k], ri_s.at[o, k], ri_in.at[r, k], (row_peer(o), c, d),
                 inside if k == moved else None)

    def forward_li(o, k):
        skip = 1 if k == moved else 0
        far = c + o
        cond = jnp.logical_and(far < C, c >= skip)
        arrive(lig.at[far, k], li_l.at[o, k], li_in.at[far, k], cond)
        if o < C - 1:
            copy(lig.at[far, k], lig.at[far, k], li_l.at[o, k], li_in.at[far, k],
                 (r, c - 1, d), jnp.logical_and(cond, c > skip))
        near = c - o
        cond = jnp.logical_and(near >= 0, c < C - skip)
        arrive(lig.at[near, k], li_r.at[o, k], li_in.at[near, k], cond)
        if o < C - 1:
            copy(lig.at[near, k], lig.at[near, k], li_r.at[o, k], li_in.at[near, k],
                 (r, c + 1, d), jnp.logical_and(cond, c < C - 1 - skip))

    half = (K + 1) // 2
    for k in range(half):
        send_li(k)
    for k in range(half):
        rig[r, k] = ri[k].T
        send_ri(k)

    ct_rows = ct[...].T
    for k in range(K):
        tp[k] = mm(ct_rows, lo[k]).astype(BF16)
    for o in range(1, C):
        n = col_peer(o)
        copy(tp.at[pl.ds(n * KC, KC)], tpr.at[c], tp_s.at[o], tp_in.at[c], (r, n, d))
    rt_rows = rt[...].T
    for k in range(K):
        pp[k] = mm(rt_rows, ro[k])
    for o in range(1, R):
        n = row_peer(o)
        copy(pp.at[pl.ds(n * KR, KR)], ppr.at[r], pp_s.at[o], pp_in.at[r], (n, c, d))
    for k in range(half, K):
        send_li(k)
    for k in range(half, K):
        rig[r, k] = ri[k].T
        send_ri(k)
    lig[c] = li[...]

    for k in range(K):
        forward_li(1, k)

    if moved < K:
        arrive(ext.at[r], ext_s.at[0], ext_in.at[r], helper)
        for o in range(1, R):
            copy(ext.at[r], ext.at[r], ext_s.at[o], ext_in.at[r], (row_peer(o), c, d), helper)

    total = tp[pl.ds(c * KC, KC)].astype(F32)
    for o in range(1, C):
        n = col_peer(o)
        arrive(tpr.at[n], tp_s.at[o], tp_in.at[n])
        total = total + tpr[n].astype(F32)
    test[c] = total.astype(BF16)
    for o in range(1, C):
        copy(test.at[c], test.at[c], te_s.at[o], te_in.at[c], (r, col_peer(o), d))
    total = pp[pl.ds(r * KR, KR)]
    for o in range(1, R):
        n = row_peer(o)
        arrive(ppr.at[n], pp_s.at[o], pp_in.at[n])
        total = total + ppr[n]
    probe[r] = total.astype(BF16)
    for o in range(1, R):
        copy(probe.at[r], probe.at[r], pr_s.at[o], pr_in.at[r], (row_peer(o), c, d))

    for o in range(2, C - 1):
        for k in range(K):
            forward_li(o, k)

    for k in range(K):
        for o in range(1, R):
            n = row_peer(o)
            arrive(rig.at[n, k], ri_s.at[o, k], ri_in.at[n, k], inside if k == moved else None)

    def cross_of(block, k):
        total = None
        for b in range(C):
            term = mm(block(b), lig[b, k])
            total = term if total is None else total + term
        return total.astype(BF16)

    if moved < K:
        for o in range(1, R):
            n = row_peer(o)
            arrive(ext.at[n], ext_s.at[o], ext_in.at[n], helper)

        @pl.when(helper)
        def _():
            xs[...] = cross_of(lambda b: ext[b], moved)

        copy(xs, xr, x_s.at[0], x_s.at[1], (r, served, d), helper)

        @pl.when(inside)
        def _():
            cx[...] = cross_of(lambda b: rig[b, moved], moved)

    for o in range(1, R):
        n = row_peer(o)
        arrive(probe.at[n], pr_s.at[o], pr_in.at[n])
    for o in range(1, C):
        n = col_peer(o)
        arrive(test.at[n], te_s.at[o], te_in.at[n])

    scale = (K * D) ** -0.5
    core_left = []
    core_part = None
    for k in range(K):
        if C > 2:
            forward_li(C - 1, k)
        if k == moved:
            arrive(xr, x_s.at[0], x_s.at[1], at_end)

            @pl.when(at_end)
            def _():
                cx[...] = xr[...]

            cross = cx[...]
        else:
            cross = cross_of(lambda b: rig[b, k], k)
        weight = mask[0, 0, k].astype(F32) * scale
        right = (mm(probe[k // KR, k % KR], cross) * weight).astype(BF16)
        lanes = pl.ds(k * rank, rank)
        crt[c, :, lanes] = right
        for o in range(1, C):
            copy(crt.at[c, :, lanes], crt.at[c, :, lanes], cr_s.at[o, k], cr_in.at[c, k],
                 (r, col_peer(o), d))
        test_k = test[k // KC, k % KC]
        core_left.append((mm(cross, test_k, (1, 1)) * weight).astype(BF16))
        term = mm(right, test_k, (1, 1))
        core_part = term if core_part is None else core_part + term

    cps[...] = core_part
    for o in range(1, D):
        copy(cps, cpr.at[d], cp_s.at[o], cp_in.at[d], (r, c, depth_peer(o)))
    cpr[d] = core_part
    for o in range(1, D):
        n = depth_peer(o)
        arrive(cpr.at[n], cp_s.at[o], cp_in.at[n])
    core = cpr[0]
    for n in range(1, D):
        core = core + cpr[n]

    gram = mm(core, core, (1, 1), HIGHEST)
    eye = (
        lax.broadcasted_iota(jnp.int32, (rank, rank), 0)
        == lax.broadcasted_iota(jnp.int32, (rank, rank), 1)
    ).astype(F32)
    trace = jnp.sum(gram * eye)
    ridge = 0.05 * trace / rank + 1e-05
    gram = gram + ridge * eye
    start, scales = inverse_schedule(rank)
    first = start / jnp.broadcast_to(trace + ridge, (rank, rank))
    inv = (scales[0] * first) * (2.0 * eye - first * gram)
    for factor in scales[1:]:
        step = 2.0 * eye - mm(gram, inv, precision=HIGHEST)
        inv = factor * mm(inv, step, precision=HIGHEST)
    weights = (mm(inv, core, precision=HIGHEST) * rank**0.5).astype(BF16)

    for k in range(K):
        rows = pl.ds(k * rank, rank)
        zz[r, rows] = mm(core_left[k], weights, (1, 1)).astype(BF16)
        for o in range(1, R):
            copy(zz.at[r, rows], zz.at[r, rows], z_s.at[o, k], z_in.at[r, k], (row_peer(o), c, d))

    part_l = lo.shape[1] // D
    place = c * D + d
    owner, slot = place // C, lax.rem(place, C)
    lo_all = jnp.concatenate([lo[k] for k in range(K)], axis=1)
    for o in range(C):
        j = col_peer(o)
        if o > 0:
            for k in range(K):
                lanes = pl.ds(k * rank, rank)
                arrive(crt.at[j, :, lanes], cr_s.at[o, k], cr_in.at[j, k])
        total = mm(lo_all, crt[j], (1, 1))
        for n in range(D):
            rps[n, j] = total[n * part_l:(n + 1) * part_l]
        for e in range(1, D):
            n = depth_peer(e)
            copy(rps.at[n, j], rpr.at[d, j], rp_s.at[e, o], rp_in.at[d, j], (r, c, n))
    for o in range(C):
        j = col_peer(o)
        total = rps[d, j]
        for e in range(1, D):
            n = depth_peer(e)
            arrive(rpr.at[n, j], rp_s.at[e, o], rp_in.at[n, j])
            total = total + rpr[n, j]
        rsend[j] = total.astype(BF16)
        copy(rsend.at[j], rout.at[slot], ro_s.at[o], ro_in.at[slot], (r, j, owner),
             owner != d if o == 0 else None)

    part_r = ro.shape[1] // D
    place_q = r * D + d
    owner_q, slot_q = place_q // R, lax.rem(place_q, R)
    ro_all = jnp.concatenate([ro[k] for k in range(K)], axis=1)
    for o in range(R):
        i = row_peer(o)
        if o > 0:
            for k in range(K):
                rows = pl.ds(k * rank, rank)
                arrive(zz.at[i, rows], z_s.at[o, k], z_in.at[i, k])
        total = mm(ro_all, zz[i])
        for n in range(D):
            qps[n, i] = total[n * part_r:(n + 1) * part_r]
        for e in range(1, D):
            n = depth_peer(e)
            copy(qps.at[n, i], qpr.at[d, i], qp_s.at[e, o], qp_in.at[d, i], (r, c, n))
    for o in range(R):
        i = row_peer(o)
        total = qps[d, i]
        for e in range(1, D):
            n = depth_peer(e)
            arrive(qpr.at[n, i], qp_s.at[e, o], qp_in.at[n, i])
            total = total + qpr[n, i]
        qsend[i] = total.astype(BF16)
        copy(qsend.at[i], qout.at[slot_q], qo_s.at[o], qo_in.at[slot_q], (i, c, owner_q),
             owner_q != d if o == 0 else None)

    @pl.when(owner == d)
    def _():
        rout[slot] = rsend[c]

    @pl.when(owner_q == d)
    def _():
        qout[slot_q] = qsend[r]

    for q in range(C):
        src = d * C + q
        mine = jnp.logical_and(src // D == c, lax.rem(src, D) == d)
        arrive(rout.at[q], ro_s.at[0], ro_in.at[q], jnp.logical_not(mine))
        out_range[q * part_l:(q + 1) * part_l, :] = rout[q]
    for q in range(R):
        src = d * R + q
        mine = jnp.logical_and(src // D == r, lax.rem(src, D) == d)
        arrive(qout.at[q], qo_s.at[0], qo_in.at[q], jnp.logical_not(mine))
        out_corange[q * part_r:(q + 1) * part_r, :] = qout[q]
    for cond, op in pending:
        guarded(cond, op.wait_send)


def body(sizes, left_outer, left_inner, right_outer, right_inner, range_test, corange_test, product_mask):
    R, C, D = sizes
    K, BL, rank = left_outer.shape[1:]
    BR = right_outer.shape[2]
    sketch = corange_test.shape[2]
    assert R == C and K % R == 0 and BL % D == 0
    KR, KC = K // R, K // C
    dma = pltpu.SemaphoreType.DMA
    vmem = pltpu.VMEM
    scratch = [
        vmem((C, K, BL, rank), BF16),
        vmem((R, K, rank, BR), BF16),
        vmem((K, rank, rank), F32),
        vmem((R, KR, rank, rank), F32),
        vmem((R, KR, rank, rank), BF16),
        vmem((K, sketch, rank), BF16),
        vmem((C, KC, sketch, rank), BF16),
        vmem((C, KC, sketch, rank), BF16),
        vmem((C, rank, K * rank), BF16),
        vmem((rank, sketch), F32),
        vmem((D, rank, sketch), F32),
        vmem((R, K * rank, rank), BF16),
        vmem((D, C, BL // D, rank), F32),
        vmem((D, C, BL // D, rank), F32),
        vmem((C, BL // D, rank), BF16),
        vmem((C, BL // D, rank), BF16),
        vmem((D, R, BR // D, rank), F32),
        vmem((D, R, BR // D, rank), F32),
        vmem((R, BR // D, rank), BF16),
        vmem((R, BR // D, rank), BF16),
        vmem((R, rank, BR), BF16),
        vmem((rank, rank), BF16),
        vmem((rank, rank), BF16),
        vmem((rank, rank), BF16),
        dma((C, K)), dma((C, K)), dma((C, K)), dma((R, K)), dma((R, K)),
        dma((R,)), dma((R,)), dma((R,)), dma((R,)),
        dma((C,)), dma((C,)), dma((C,)), dma((C,)),
        dma((C, K)), dma((C, K)), dma((D,)), dma((D,)), dma((R, K)), dma((R, K)),
        dma((D, C)), dma((D, C)), dma((C,)), dma((C,)),
        dma((D, R)), dma((D, R)), dma((R,)), dma((R,)),
        dma((R,)), dma((R,)), dma((2,)),
    ]
    tile = BL * C
    whole = pl.BlockSpec(memory_space=pltpu.VMEM)
    out = jax.ShapeDtypeStruct((tile // D, rank), BF16)
    range_rows, corange_rows = pl.pallas_call(
        functools.partial(kernel, (R, C, D, K)),
        out_shape=(out, out),
        in_specs=[whole] * 6 + [pl.BlockSpec(memory_space=pltpu.SMEM)],
        out_specs=(whole, whole),
        scratch_shapes=scratch,
        compiler_params=pltpu.CompilerParams(
            collective_id=0, has_side_effects=True, vmem_limit_bytes=60 * 1024 * 1024
        ),
    )(left_outer[0], left_inner[0], right_outer[0], right_inner[0],
      range_test[0], corange_test[0], product_mask)
    return range_rows[None, None].astype(F32), corange_rows[None, None].astype(F32)


def solution(mesh):
    sizes = tuple(mesh.shape[name] for name in ("row", "col", "depth"))
    return jax.shard_map(
        functools.partial(body, sizes),
        mesh=mesh,
        in_specs=(
            P("row", "depth", "col", None),
            P("row", "depth", "col", None),
            P("col", "depth", "row", None),
            P("col", "depth", "row", None),
            P("col", "row", None),
            P("row", "col", None),
            P("row", "col", "depth"),
        ),
        out_specs=(P("row", "col", "depth", None), P("row", "col", "depth", None)),
        check_vma=False,
    )
```
